32 devices in a mesh: subtree: 4 (over y, core), tile: 8 (over z, x).
Axes of the slice: x: 2, y: 2, z: 4, core: 2. Of those that a mesh axis runs over, the one named last changes fastest.
Arguments:
- interface_stiffness: float32 [4, 4096, 4096], P('subtree', 'tile'), may hold values from -3 to 3
- lower_factor: bfloat16 [4, 4096, 512], P('subtree', 'tile'), may hold values from -0.25 to 0.25
- upper_factor: bfloat16 [4, 512, 4096], P('subtree', None, 'tile'), may hold values from -6 to 6
- modes: bfloat16 [4096, 256], P('tile'), may hold values from -0.09375 to 0.09375
- gyro_rows: int32 [512], replicated, may hold values from 0 to 4095, as said below
- gyro_coupling: float32 [512, 512], replicated, may hold values from -24 to 24
- spin_softening: float32 [512], replicated, may hold values from 0.5 to 8
- speed_index: int32 [2], replicated, may hold values from 0 to 63
Outputs:
- schur: float32 [4096, 4096], P('tile', 'subtree')
- campbell: float32 [2, 256, 256], P(None, 'tile', 'subtree')
The draws below stay inside these ranges and needn't reach their ends.
Inputs may be any that keep to these rules, and one draw needn't show every extreme that they name: `gyro_rows`: distinct interface degrees of freedom, in whole aligned blocks of 8 consecutive ones.
All inputs are finite; a program needn't handle non-finite values.
Results may differ from the reference program's by a relative error of at most 0.0003.
Values may be sent and summed in bfloat16 or wider, within the bound.
No kernel may reach another device: no remote copies, remote signals or barrier semaphores. Data moves between devices by JAX's collectives and lax.ppermute only.
A program may use at most 64 MiB of HBM per device.

```python
import math
import jax
import jax.numpy as jnp
from jax import lax

NI = 4096
SEP = 512
LEAVES = 1
MODES = 256
GYRO = 512
SPEED_STEPS = 64
SPEEDS = 2
BRANCHES = 4


def draw_gyro_rows(key, part):
    block_count = NI // 8
    chosen_count = GYRO // 8
    middle = jax.random.permutation(key, block_count - 2)[:chosen_count - 2] + 1
    blocks = jnp.concatenate([jnp.zeros((1,), jnp.int32), middle.astype(jnp.int32), jnp.full((1,), block_count - 1, jnp.int32)])
    shuffle = jax.random.permutation(jax.random.fold_in(key, 7), chosen_count)
    blocks = blocks[shuffle]
    dof_rows = blocks[:, None] * 8 + jnp.arange(8, dtype=jnp.int32)[None, :]
    return dof_rows.reshape(-1).astype(jnp.int32)


def block_levels(rng, shape, split, smallest, largest):
    factor_of = 1.0
    for axis_at, shards_of in split:
        draws = jax.random.uniform(jax.random.fold_in(jax.random.fold_in(rng, 6), axis_at), (shards_of,), jnp.float32, smallest / len(split), largest / len(split))
        factor_of = factor_of * jnp.repeat(jnp.exp(draws), shape[axis_at] // shards_of).reshape((-1,) + (1,) * (len(shape) - 1 - axis_at))
    return factor_of


def bell_draw(own_key, extent, scale, reach, split=(), kind=jnp.bfloat16):
    entries = scale * jax.random.normal(own_key, extent, jnp.float32)
    if split:
        entries = entries * block_levels(own_key, extent, split, -0.22, 0.18)
    return jnp.clip(entries, -reach, reach).astype(kind)


def setup_inputs(seed: int = 0) -> dict:
    arg_keys = jax.random.split(jax.random.key(seed), 9)
    interface_stiffness = bell_draw(arg_keys[0], (BRANCHES, NI, NI), 0.5, 3.0, ((0, 4), (1, 8)), jnp.float32)
    lower_factor = bell_draw(arg_keys[1], (BRANCHES, NI, SEP), (LEAVES * SEP) ** -0.5, 0.25, ((0, 4), (1, 8)))
    upper_factor = bell_draw(arg_keys[2], (BRANCHES, SEP, NI), 1.0, 6.0, ((0, 4), (2, 8)))
    modes = bell_draw(arg_keys[3], (NI, MODES), NI ** -0.5, 0.09375, ((0, 8),))
    gyro_rows = draw_gyro_rows(jax.random.fold_in(arg_keys[8], 71), 0)
    gyro_coupling = bell_draw(arg_keys[5], (GYRO, GYRO), 4.0, 24.0, (), jnp.float32)
    spin_softening = jnp.clip(jnp.exp(jax.random.uniform(arg_keys[6], (GYRO,), jnp.float32, math.log(0.5), math.log(8.0))), 0.5, 8.0)
    speed_index = jax.random.randint(arg_keys[7], (SPEEDS,), 0, SPEED_STEPS).astype(jnp.int32)
    return dict(interface_stiffness=interface_stiffness, lower_factor=lower_factor, upper_factor=upper_factor, modes=modes, gyro_rows=gyro_rows, gyro_coupling=gyro_coupling, spin_softening=spin_softening, speed_index=speed_index)


OMEGA_TOP = 2.0


def reference(interface_stiffness, lower_factor, upper_factor, modes, gyro_rows, gyro_coupling, spin_softening, speed_index):
    stacked_lower = jnp.moveaxis(lower_factor, 0, 1).reshape(NI, BRANCHES * SEP)
    stacked_upper = upper_factor.reshape(BRANCHES * SEP, NI)
    coupled = jnp.dot(stacked_lower, stacked_upper, preferred_element_type=jnp.float32)
    schur = jnp.sum(interface_stiffness, axis=0) - coupled
    wide_modes = modes.astype(jnp.float32)
    response = jnp.dot(schur, wide_modes, precision=lax.Precision.HIGHEST, preferred_element_type=jnp.float32)
    stiffness = jnp.dot(wide_modes.T, response, precision=lax.Precision.HIGHEST, preferred_element_type=jnp.float32)
    picked = jnp.take(modes, gyro_rows.astype(jnp.int32), axis=0).astype(jnp.float32)
    skew_part = 0.5 * (gyro_coupling - gyro_coupling.T)
    turned = jnp.dot(skew_part, picked, precision=lax.Precision.HIGHEST, preferred_element_type=jnp.float32)
    gyro_block = jnp.dot(picked.T, turned, precision=lax.Precision.HIGHEST, preferred_element_type=jnp.float32)
    spin_block = jnp.dot(picked.T, spin_softening[:, None] * picked, precision=lax.Precision.HIGHEST, preferred_element_type=jnp.float32)
    speeds_omega = OMEGA_TOP * (speed_index.astype(jnp.float32) + 1.0) / SPEED_STEPS
    campbell = stiffness[None] + speeds_omega[:, None, None] * gyro_block[None] - (speeds_omega * speeds_omega)[:, None, None] * spin_block[None]
    return schur, campbell
```

```python
import jax
import jax.numpy as jnp
from jax import lax
from jax.sharding import PartitionSpec as P

SPEED_STEPS = 64


OMEGA_TOP = 2.0

SHARE_SCALE = 32.0


def omegas(speed_index):
    return OMEGA_TOP * (speed_index.astype(jnp.float32) + 1.0) / SPEED_STEPS


def combine(stiff_block, gyro_block, spin_block, speed_index):
    speeds_omega = omegas(speed_index)
    return (
        stiff_block[None]
        + speeds_omega[:, None, None] * gyro_block[None]
        - (speeds_omega * speeds_omega)[:, None, None] * spin_block[None]
    )


def gyro_parts(picked, gyro_coupling, spin_softening, left_first, left_count, right_first, right_count):
    skew_part = 0.5 * (gyro_coupling - gyro_coupling.T)
    left_modes = lax.dynamic_slice_in_dim(picked, left_first, left_count, 1)
    right_modes = lax.dynamic_slice_in_dim(picked, right_first, right_count, 1)
    turned = jnp.dot(
        skew_part, right_modes, precision=lax.Precision.HIGHEST, preferred_element_type=jnp.float32
    )
    gyro_block = jnp.einsum(
        "gm,gc->mc",
        left_modes,
        turned,
        precision=lax.Precision.HIGHEST,
        preferred_element_type=jnp.float32,
    )
    spin_block = jnp.einsum(
        "gm,gc->mc",
        left_modes,
        spin_softening[:, None] * right_modes,
        precision=lax.Precision.HIGHEST,
        preferred_element_type=jnp.float32,
    )
    return gyro_block, spin_block


def partner(block, axis, distance):
    count = lax.axis_size(axis)
    route = []
    for low in range(count):
        high = low | 1 << distance
        if high != low and high < count:
            route += [(low, high), (high, low)]
    return lax.ppermute(block, axis, route)


def shards_any(
    interface_stiffness,
    lower_factor,
    upper_factor,
    modes,
    gyro_rows,
    gyro_coupling,
    spin_softening,
    speed_index,
):
    tile_count = lax.axis_size("tile")
    branch_count = lax.axis_size("subtree")
    tile_pos = lax.axis_index("tile")
    branch_pos = lax.axis_index("subtree")
    mode_count = modes.shape[1]
    mode_cols = mode_count // branch_count
    mode_rows_dev = mode_count // tile_count
    coupled = jnp.einsum(
        "lrk,lkn->rn",
        lower_factor,
        lax.all_gather(upper_factor, "tile", axis=2, tiled=True),
        preferred_element_type=jnp.float32,
    )
    schur_part = jnp.sum(interface_stiffness, axis=0) - coupled
    own_width = schur_part.shape[1] // branch_count
    for level_bit in range(branch_count.bit_length() - 1):
        schur_part = schur_part + partner(schur_part, "subtree", level_bit)
    schur_out = lax.dynamic_slice_in_dim(schur_part, branch_pos * own_width, own_width, 1)
    segment = lax.all_gather(modes, "tile", axis=0, tiled=True)
    wanted = lax.dynamic_slice_in_dim(segment, branch_pos * mode_cols, mode_cols, 1)
    response = jnp.dot(
        schur_part,
        wanted.astype(jnp.float32),
        precision=lax.Precision.HIGHEST,
        preferred_element_type=jnp.float32,
    )
    partial_value = jnp.einsum(
        "rm,rc->mc",
        modes.astype(jnp.float32),
        response,
        precision=lax.Precision.HIGHEST,
        preferred_element_type=jnp.float32,
    )
    stiff_block = lax.psum_scatter(partial_value, "tile", scatter_dimension=0, tiled=True)
    picked = jnp.take(segment, gyro_rows, axis=0, mode="clip").astype(jnp.float32)
    gyro_block, spin_block = gyro_parts(
        picked,
        gyro_coupling,
        spin_softening,
        tile_pos * mode_rows_dev,
        mode_rows_dev,
        branch_pos * mode_cols,
        mode_cols,
    )
    return (schur_out, combine(stiff_block, gyro_block, spin_block, speed_index))


def shards_ring(
    interface_stiffness,
    lower_factor,
    upper_factor,
    modes,
    gyro_rows,
    gyro_coupling,
    spin_softening,
    speed_index,
):
    f32 = jnp.float32
    tiles = lax.axis_size("tile")
    branches = lax.axis_size("subtree")
    tile = lax.axis_index("tile")
    branch = lax.axis_index("subtree")
    z, x = tile // 2, tile % 2
    y, core = branch // 2, branch % 2
    stiffness = interface_stiffness[0]
    lower = lower_factor[0]
    upper = upper_factor[0]
    rows, width = stiffness.shape
    depth, cols = upper.shape
    mode_count = modes.shape[1]

    def gray(i):
        return i ^ (i >> 1)

    def over_z(block):
        step = [(gray(p) * 2 + a, gray((p + 1) % 4) * 2 + a) for p in range(4) for a in range(2)]
        return lax.ppermute(block, "tile", step)

    def over_x(block):
        return lax.ppermute(block, "tile", [(i, i ^ 1) for i in range(tiles)])

    def over_y(block):
        return lax.ppermute(block, "subtree", [(i, i ^ 2) for i in range(branches)])

    def over_core(block):
        return lax.ppermute(block, "subtree", [(i, i ^ 1) for i in range(branches)])

    from_z = [gray((gray(z) - k) % 4) for k in range(4)]
    from_x = [x, 1 - x]

    chunk = modes.shape[0] // branches
    mine = lax.dynamic_slice_in_dim(modes, branch * chunk, chunk, 0)
    mode_z = [mine]
    for _ in range(3):
        mode_z.append(over_z(mode_z[-1]))
    mode_own = jnp.stack(mode_z)
    mode_other = over_x(mode_own)
    quarter = jnp.zeros((4, 2, chunk, mode_count), modes.dtype)
    for k in range(4):
        for j, source in enumerate((mode_own, mode_other)):
            quarter = lax.dynamic_update_slice(
                quarter, source[k][None, None], (from_z[k], from_x[j], 0, 0)
            )
    quarter = quarter.reshape(tiles, chunk, mode_count)
    across = over_y(quarter)
    half = jnp.stack(
        [jnp.where(y == 0, quarter, across), jnp.where(y == 0, across, quarter)], axis=1
    )
    beside = over_core(half)
    all_modes = jnp.stack(
        [jnp.where(core == 0, half, beside), jnp.where(core == 0, beside, half)], axis=2
    ).reshape(tiles * modes.shape[0], mode_count)

    z1, x0 = lax.optimization_barrier((over_z(upper), over_x(upper)))
    z2, x1 = lax.optimization_barrier((over_z(z1), over_x(z1)))
    z3, x2 = lax.optimization_barrier((over_z(z2), over_x(z2)))
    cut = depth // 2
    x3_low, x3_high = over_x(z3[:cut]), over_z(x2[cut:])

    def first_col(k, j):
        return (from_z[k] * 2 + from_x[j]) * cols

    def share(k, j, product):
        return lax.dynamic_slice_in_dim(stiffness, first_col(k, j), cols, 1) - product

    def times(left, right):
        return jnp.dot(left, right, preferred_element_type=f32)

    parts = [
        [share(k, 0, times(lower, block)) for k, block in enumerate((upper, z1, z2, z3))],
        [share(k, 1, times(lower, block)) for k, block in enumerate((x0, x1, x2))],
    ]
    parts[1].append(share(3, 1, times(lower[:, :cut], x3_low) + times(lower[:, cut:], x3_high)))

    response = jnp.zeros((rows, mode_count), f32)
    for j in range(2):
        for k in range(4):
            block_modes = lax.dynamic_slice_in_dim(all_modes, first_col(k, j), cols, 0)
            response = response + jnp.dot(
                parts[j][k],
                block_modes.astype(f32),
                precision=lax.Precision.HIGH,
                preferred_element_type=f32,
            )
    reduced = jnp.einsum(
        "rm,rc->mc",
        modes.astype(f32),
        response,
        precision=lax.Precision.HIGH,
        preferred_element_type=f32,
    )
    mode_rows = mode_count // tiles
    mode_cols = mode_count // branches
    pieces = reduced.reshape(tiles, mode_rows, branches, mode_cols).transpose(2, 0, 1, 3)
    pieces = pieces.reshape(branches * tiles, mode_rows, mode_cols)
    pieces = lax.all_to_all(pieces, ("subtree", "tile"), 0, 0)
    stiff_block = jnp.sum(pieces, axis=0)

    final = []
    keep_first = [from_z[k] % 2 == core for k in range(2)]
    kept_z = [jnp.where(keep_first[k], from_z[k], from_z[k + 2]) for k in range(2)]
    stays = kept_z[0] // 2 == y
    for j in range(2):
        both = []
        for k in range(2):
            kept = jnp.where(keep_first[k], parts[j][k], parts[j][k + 2])
            sent = jnp.where(keep_first[k], parts[j][k + 2], parts[j][k])
            both.append(kept + over_core(sent))
        sent = jnp.where(stays, both[1], both[0])
        arrived = over_y((sent * SHARE_SCALE).astype(jnp.float16))
        final.append(
            jnp.where(stays, both[0], both[1]) + arrived.astype(f32) * (1.0 / SHARE_SCALE)
        )
    schur_out = jnp.concatenate(
        [jnp.where(x == 0, final[0], final[1]), jnp.where(x == 0, final[1], final[0])], axis=1
    )

    picked = jnp.take(all_modes, gyro_rows, axis=0, mode="clip").astype(f32)
    gyro_block, spin_block = gyro_parts(
        picked,
        gyro_coupling,
        spin_softening,
        tile * mode_rows,
        mode_rows,
        branch * mode_cols,
        mode_cols,
    )
    return (schur_out, combine(stiff_block, gyro_block, spin_block, speed_index))


def solution(mesh):
    placed = (
        P("subtree", "tile", None),
        P("subtree", "tile", None),
        P("subtree", None, "tile"),
        P("tile", None),
        P(),
        P(),
        P(),
        P(),
    )
    ring = (mesh.shape["subtree"], mesh.shape["tile"]) == (4, 8)
    return jax.shard_map(
        shards_ring if ring else shards_any,
        mesh=mesh,
        in_specs=placed,
        out_specs=(P("tile", "subtree"), P(None, "tile", "subtree")),
        check_vma=False,
    )
```

```python
import jax
import jax.numpy as jnp
from jax import lax
from jax.experimental import pallas as pl
from jax.experimental.pallas import tpu as pltpu
from jax.sharding import PartitionSpec as P

SPEED_STEPS = 64


OMEGA_TOP = 2.0

SHARE_SCALE = 32.0


def omegas(speed_index):
    return OMEGA_TOP * (speed_index.astype(jnp.float32) + 1.0) / SPEED_STEPS


def combine(stiff_block, gyro_block, spin_block, speed_index):
    speeds_omega = omegas(speed_index)
    return (
        stiff_block[None]
        + speeds_omega[:, None, None] * gyro_block[None]
        - (speeds_omega * speeds_omega)[:, None, None] * spin_block[None]
    )


def gyro_parts(picked, gyro_coupling, spin_softening, left_first, left_count, right_first, right_count):
    skew_part = 0.5 * (gyro_coupling - gyro_coupling.T)
    left_modes = lax.dynamic_slice_in_dim(picked, left_first, left_count, 1)
    right_modes = lax.dynamic_slice_in_dim(picked, right_first, right_count, 1)
    turned = jnp.dot(
        skew_part, right_modes, precision=lax.Precision.HIGHEST, preferred_element_type=jnp.float32
    )
    gyro_block = jnp.einsum(
        "gm,gc->mc",
        left_modes,
        turned,
        precision=lax.Precision.HIGHEST,
        preferred_element_type=jnp.float32,
    )
    spin_block = jnp.einsum(
        "gm,gc->mc",
        left_modes,
        spin_softening[:, None] * right_modes,
        precision=lax.Precision.HIGHEST,
        preferred_element_type=jnp.float32,
    )
    return gyro_block, spin_block


def partner(block, axis, distance):
    count = lax.axis_size(axis)
    route = []
    for low in range(count):
        high = low | 1 << distance
        if high != low and high < count:
            route += [(low, high), (high, low)]
    return lax.ppermute(block, axis, route)


def shards_any(
    interface_stiffness,
    lower_factor,
    upper_factor,
    modes,
    gyro_rows,
    gyro_coupling,
    spin_softening,
    speed_index,
):
    tile_count = lax.axis_size("tile")
    branch_count = lax.axis_size("subtree")
    tile_pos = lax.axis_index("tile")
    branch_pos = lax.axis_index("subtree")
    mode_count = modes.shape[1]
    mode_cols = mode_count // branch_count
    mode_rows_dev = mode_count // tile_count
    coupled = jnp.einsum(
        "lrk,lkn->rn",
        lower_factor,
        lax.all_gather(upper_factor, "tile", axis=2, tiled=True),
        preferred_element_type=jnp.float32,
    )
    schur_part = jnp.sum(interface_stiffness, axis=0) - coupled
    own_width = schur_part.shape[1] // branch_count
    for level_bit in range(branch_count.bit_length() - 1):
        schur_part = schur_part + partner(schur_part, "subtree", level_bit)
    schur_out = lax.dynamic_slice_in_dim(schur_part, branch_pos * own_width, own_width, 1)
    segment = lax.all_gather(modes, "tile", axis=0, tiled=True)
    wanted = lax.dynamic_slice_in_dim(segment, branch_pos * mode_cols, mode_cols, 1)
    response = jnp.dot(
        schur_part,
        wanted.astype(jnp.float32),
        precision=lax.Precision.HIGHEST,
        preferred_element_type=jnp.float32,
    )
    partial_value = jnp.einsum(
        "rm,rc->mc",
        modes.astype(jnp.float32),
        response,
        precision=lax.Precision.HIGHEST,
        preferred_element_type=jnp.float32,
    )
    stiff_block = lax.psum_scatter(partial_value, "tile", scatter_dimension=0, tiled=True)
    picked = jnp.take(segment, gyro_rows, axis=0, mode="clip").astype(jnp.float32)
    gyro_block, spin_block = gyro_parts(
        picked,
        gyro_coupling,
        spin_softening,
        tile_pos * mode_rows_dev,
        mode_rows_dev,
        branch_pos * mode_cols,
        mode_cols,
    )
    return (schur_out, combine(stiff_block, gyro_block, spin_block, speed_index))


def gray(i):
    return i ^ (i >> 1)


def ring_z(place, k):
    return gray((gray(place[0] >> 1) + (4 - k)) & 3)


def block_at(place, j, k):
    return ring_z(place, k) * 2 + ((place[0] & 1) ^ j)


def keeps(place, k):
    return (ring_z(place, k) & 1) == (place[1] & 1)


def stays(place):
    kept_z = jnp.where(keeps(place, 0), ring_z(place, 0), ring_z(place, 2))
    return (kept_z >> 1) == (place[1] >> 1)


def whole(shape):
    return pl.BlockSpec(shape, lambda *_: (0,) * len(shape))


def call(body, grid, in_specs, out_specs, out_shape, flops, moved, scratch=()):
    return pl.pallas_call(
        body,
        out_shape=out_shape,
        grid_spec=pltpu.PrefetchScalarGridSpec(
            num_scalar_prefetch=1,
            grid=grid,
            in_specs=in_specs,
            out_specs=out_specs,
            scratch_shapes=scratch,
        ),
        compiler_params=pltpu.CompilerParams(vmem_limit_bytes=40 << 20),
        cost_estimate=pl.CostEstimate(flops=flops, bytes_accessed=moved, transcendentals=0),
    )


def mul(left, right):
    return jnp.dot(left, right, preferred_element_type=jnp.float32)


def mul_wide(left, right):
    high = left.astype(jnp.bfloat16)
    low = (left - high.astype(jnp.float32)).astype(jnp.bfloat16)
    return mul(high, right) + mul(low, right)


def shares(place, stiffness, lower, blocks, first):
    rows = stiffness.shape[0]
    depth, cols = blocks[0][2].shape
    step = rows // 2
    steps = rows // step
    count = len(blocks)
    pairs = [f for f in first if f is not None]

    def stiff_spec(j, k):
        return pl.BlockSpec((step, cols), lambda i, at: (i, block_at(at, j, k)))

    tile_spec = pl.BlockSpec((step, cols), lambda i, at: (i, 0))
    in_specs = [stiff_spec(j, k) for j, k, _ in blocks]
    in_specs += [pl.BlockSpec((step, depth), lambda i, at: (i, 0))]
    in_specs += [whole((depth, cols))] * count + [tile_spec] * len(pairs)
    outs = count + len(pairs)

    def body(at, *refs):
        stiff = refs[:count]
        low = refs[count][...]
        uppers = refs[count + 1 : 2 * count + 1]
        olds = list(refs[2 * count + 1 : 2 * count + 1 + len(pairs)])
        outputs = list(refs[2 * count + 1 + len(pairs) :])
        for n, (j, k, _) in enumerate(blocks):
            value = stiff[n][...] - mul(low, uppers[n][...])
            if first[n] is None:
                outputs.pop(0)[...] = value
                continue
            old = olds.pop(0)
            sent, kept = outputs.pop(0), outputs.pop(0)
            keep_old = keeps(at, k - 2)

            @pl.when(keep_old)
            def _():
                sent[...] = value
                kept[...] = old[...]

            @pl.when(jnp.logical_not(keep_old))
            def _():
                sent[...] = old[...]
                kept[...] = value

    return call(
        body,
        (steps,),
        in_specs,
        [tile_spec] * outs,
        [jax.ShapeDtypeStruct((rows, cols), jnp.float32)] * outs,
        2 * count * rows * cols * depth,
        4 * rows * cols * (count + outs),
    )(place, *[stiffness] * count, lower, *[b[2] for b in blocks], *pairs)


def fill_modes(at, target, near, beside, j, k):
    chunk = near.shape[2]
    for dist in range(4):
        source = beside if dist % 2 else near
        first = pl.multiple_of((at[1] ^ dist) * chunk, chunk)
        target[pl.ds(first, chunk), :] = source[dist // 2, j * 4 + k]


def respond(place, near, beside, plain, pairs):
    rows, cols = plain[0][2].shape
    modes_count = near.shape[3]
    flat = [p[2] for p in plain] + [s for p in pairs for s in p[2:]]
    step = rows // 2
    tile_spec = pl.BlockSpec((step, cols), lambda i, at: (i, 0))

    def body(at, near_ref, beside_ref, *refs):
        share_refs, out, scratch = list(refs[: len(flat)]), refs[len(flat)], refs[len(flat) + 1]
        total = jnp.zeros((step, modes_count), jnp.float32)
        order = [(j, k) for j, k, _ in plain]
        for j, k, _, _ in pairs:
            keep_old = keeps(at, k)
            order.append((j, jnp.where(keep_old, k + 2, k)))
            order.append((j, jnp.where(keep_old, k, k + 2)))
        for n, (j, k) in enumerate(order):
            fill_modes(at, scratch.at[n], near_ref, beside_ref, j, k)
            total += mul_wide(share_refs[n][...], scratch[n])
        out[...] = total

    return call(
        body,
        (rows // step,),
        [whole(near.shape), whole(beside.shape)] + [tile_spec] * len(flat),
        pl.BlockSpec((step, modes_count), lambda i, at: (i, 0)),
        jax.ShapeDtypeStruct((rows, modes_count), jnp.float32),
        4 * len(flat) * rows * cols * modes_count,
        4 * len(flat) * rows * cols,
        [pltpu.VMEM((len(flat), cols, modes_count), jnp.bfloat16)],
    )(place, near, beside, *flat)


def last_share(place, stiffness, lower, low_half, high_half, old, near, beside, response, modes):
    rows = stiffness.shape[0]
    cut, cols = low_half.shape
    depth = lower.shape[1]
    mode_count = modes.shape[1]
    branches, tiles = 4, 8
    group = mode_count // tiles // 2

    def body(at, stiff, low, lo, hi, old_ref, near_ref, beside_ref, resp, mode, sent, kept, pieces, scratch):
        fill_modes(at, scratch, near_ref, beside_ref, 1, 3)
        value = stiff[...] - mul(low[:, :cut], lo[...]) - mul(low[:, cut:], hi[...])
        keep_old = keeps(at, 1)

        @pl.when(keep_old)
        def _():
            sent[...] = value
            kept[...] = old_ref[...]

        @pl.when(jnp.logical_not(keep_old))
        def _():
            sent[...] = old_ref[...]
            kept[...] = value

        total = resp[...] + mul_wide(value, scratch[...])
        high = total.astype(jnp.bfloat16)
        rest = (total - high.astype(jnp.float32)).astype(jnp.bfloat16)
        across = (((0,), (0,)), ((), ()))
        reduced = lax.dot_general(
            mode[...], high, across, preferred_element_type=jnp.float32
        ) + lax.dot_general(mode[...], rest, across, preferred_element_type=jnp.float32)
        split = reduced.reshape(tiles, 2, group, mode_count)
        upper = split[:, 0].reshape(tiles * group, mode_count)
        under = split[:, 1].reshape(tiles * group, mode_count)
        left = lax.broadcasted_iota(jnp.int32, (tiles * group, 128), 1) < 64
        for pair in range(branches // 2):
            u = upper[:, 128 * pair : 128 * pair + 128]
            v = under[:, 128 * pair : 128 * pair + 128]
            pieces[2 * pair] = jnp.where(left, u, pltpu.roll(v, 64, 1))
            pieces[2 * pair + 1] = jnp.where(left, pltpu.roll(u, 64, 1), v)

    share_shape = jax.ShapeDtypeStruct((rows, cols), jnp.float32)
    return call(
        body,
        (1,),
        [
            pl.BlockSpec((rows, cols), lambda i, at: (0, block_at(at, 1, 3))),
            whole(lower.shape),
            whole(low_half.shape),
            whole(high_half.shape),
            whole((rows, cols)),
            whole(near.shape),
            whole(beside.shape),
            whole(response.shape),
            whole(modes.shape),
        ],
        [whole((rows, cols)), whole((rows, cols)), whole((branches, tiles * group, 128))],
        [share_shape, share_shape, jax.ShapeDtypeStruct((branches, tiles * group, 128), jnp.float32)],
        2 * rows * cols * (depth + 2 * mode_count),
        16 * rows * cols,
        [pltpu.VMEM((cols, mode_count), jnp.bfloat16)],
    )(place, stiffness, lower, low_half, high_half, old, near, beside, response, modes)


def join(place, kept, came):
    here = stays(place)
    both = [kept[n] + came[n] for n in range(2)]
    sent = jnp.where(here, both[1], both[0])
    return (sent * SHARE_SCALE).astype(jnp.float16), jnp.where(here, both[0], both[1])


def finish(place, own, came):
    first, second = (
        mine + other.astype(jnp.float32) * (1.0 / SHARE_SCALE) for mine, other in zip(own, came)
    )
    cols = first.shape[1]
    return lax.dynamic_update_slice_in_dim(
        jnp.concatenate([first, first], axis=1), second, (1 - (place[0] & 1)) * cols, 1
    )


def shards_ring(
    interface_stiffness,
    lower_factor,
    upper_factor,
    modes,
    gyro_rows,
    gyro_coupling,
    spin_softening,
    speed_index,
):
    f32 = jnp.float32
    tiles = lax.axis_size("tile")
    branches = lax.axis_size("subtree")
    tile = lax.axis_index("tile")
    branch = lax.axis_index("subtree")
    place = jnp.stack([tile, branch]).astype(jnp.int32)
    stiffness = interface_stiffness[0]
    lower = lower_factor[0]
    upper = upper_factor[0]
    mode_count = modes.shape[1]

    def over_z(block):
        step = [(gray(p) * 2 + a, gray((p + 1) % 4) * 2 + a) for p in range(4) for a in range(2)]
        return lax.ppermute(block, "tile", step)

    def over_x(block):
        return lax.ppermute(block, "tile", [(i, i ^ 1) for i in range(tiles)])

    def over_y(block):
        return lax.ppermute(block, "subtree", [(i, i ^ 2) for i in range(branches)])

    def over_core(block):
        return lax.ppermute(block, "subtree", [(i, i ^ 1) for i in range(branches)])

    chunk = modes.shape[0] // branches
    mode_z = [lax.dynamic_slice_in_dim(modes, branch * chunk, chunk, 0)]
    for _ in range(3):
        mode_z.append(over_z(mode_z[-1]))
    mode_own = jnp.stack(mode_z)
    quarter = jnp.concatenate([mode_own, over_x(mode_own)])
    near = jnp.stack([quarter, over_y(quarter)])
    beside = over_core(near)

    z1, x0 = lax.optimization_barrier((over_z(upper), over_x(upper)))
    z2, x1 = lax.optimization_barrier((over_z(z1), over_x(z1)))
    z3, x2 = lax.optimization_barrier((over_z(z2), over_x(z2)))
    cut = upper.shape[0] // 2
    x3_low, x3_high = over_x(z3[:cut]), over_z(x2[cut:])

    (p00,) = shares(place, stiffness, lower, [(0, 0, upper)], [None])
    p01, p10 = shares(place, stiffness, lower, [(0, 1, z1), (1, 0, x0)], [None, None])
    sent_a0, kept_a0, p11 = shares(place, stiffness, lower, [(0, 2, z2), (1, 1, x1)], [p00, None])
    sent_b0, kept_b0, sent_a1, kept_a1 = shares(
        place, stiffness, lower, [(0, 3, z3), (1, 2, x2)], [p01, p10]
    )
    response = respond(
        place,
        near,
        beside,
        [(1, 1, p11)],
        [(0, 0, sent_a0, kept_a0), (0, 1, sent_b0, kept_b0), (1, 0, sent_a1, kept_a1)],
    )
    sent_b1, kept_b1, pieces = last_share(
        place, stiffness, lower, x3_low, x3_high, p11, near, beside, response, modes
    )

    mode_rows = mode_count // tiles
    mode_cols = mode_count // branches
    pieces = pieces.reshape(branches * tiles, mode_rows // 2, 2 * mode_cols)
    summed = jnp.sum(lax.all_to_all(pieces, ("subtree", "tile"), 0, 0), axis=0)
    stiff_block = jnp.concatenate([summed[:, :mode_cols], summed[:, mode_cols:]], axis=0)

    own, came = [], []
    for kept, sent in (
        ((kept_a0, kept_b0), (sent_a0, sent_b0)),
        ((kept_a1, kept_b1), (sent_a1, sent_b1)),
    ):
        gone, stayed = join(place, kept, [over_core(s) for s in sent])
        own.append(stayed)
        came.append(over_y(gone))
    schur_out = finish(place, own, came)

    row_tile, row_in = gyro_rows // modes.shape[0], gyro_rows % modes.shape[0]
    dist = (row_in // chunk) ^ branch
    turn = (gray(tile // 2) - gray(row_tile // 2)) & 3
    held = ((dist & 1) * 2 + (dist >> 1)) * 8 + ((row_tile ^ tile) & 1) * 4 + turn
    table = jnp.concatenate([near, beside]).reshape(tiles * modes.shape[0], mode_count)
    picked = jnp.take(table, held * chunk + row_in % chunk, axis=0, mode="clip").astype(f32)
    gyro_block, spin_block = gyro_parts(
        picked,
        gyro_coupling,
        spin_softening,
        tile * mode_rows,
        mode_rows,
        branch * mode_cols,
        mode_cols,
    )
    return (schur_out, combine(stiff_block, gyro_block, spin_block, speed_index))


def solution(mesh):
    placed = (
        P("subtree", "tile", None),
        P("subtree", "tile", None),
        P("subtree", None, "tile"),
        P("tile", None),
        P(),
        P(),
        P(),
        P(),
    )
    ring = (mesh.shape["subtree"], mesh.shape["tile"]) == (4, 8)
    return jax.shard_map(
        shards_ring if ring else shards_any,
        mesh=mesh,
        in_specs=placed,
        out_specs=(P("tile", "subtree"), P(None, "tile", "subtree")),
        check_vma=False,
    )
```

```python
import jax
import jax.numpy as jnp
from jax import lax
from jax.experimental import pallas as pl
from jax.experimental.pallas import tpu as pltpu
from jax.sharding import PartitionSpec as P

SPEED_STEPS = 64


OMEGA_TOP = 2.0

SHARE_SCALE = 32.0

GRANT = 16 << 20


def omegas(speed_index):
    return OMEGA_TOP * (speed_index.astype(jnp.float32) + 1.0) / SPEED_STEPS


def combine(stiff_block, gyro_block, spin_block, speed_index):
    speeds_omega = omegas(speed_index)
    return (
        stiff_block[None]
        + speeds_omega[:, None, None] * gyro_block[None]
        - (speeds_omega * speeds_omega)[:, None, None] * spin_block[None]
    )


def gyro_parts(picked, gyro_coupling, spin_softening, left_first, left_count, right_first, right_count):
    skew_part = 0.5 * (gyro_coupling - gyro_coupling.T)
    left_modes = lax.dynamic_slice_in_dim(picked, left_first, left_count, 1)
    right_modes = lax.dynamic_slice_in_dim(picked, right_first, right_count, 1)
    turned = jnp.dot(
        skew_part, right_modes, precision=lax.Precision.HIGHEST, preferred_element_type=jnp.float32
    )
    gyro_block = jnp.einsum(
        "gm,gc->mc",
        left_modes,
        turned,
        precision=lax.Precision.HIGHEST,
        preferred_element_type=jnp.float32,
    )
    spin_block = jnp.einsum(
        "gm,gc->mc",
        left_modes,
        spin_softening[:, None] * right_modes,
        precision=lax.Precision.HIGHEST,
        preferred_element_type=jnp.float32,
    )
    return gyro_block, spin_block


def partner(block, axis, distance):
    count = lax.axis_size(axis)
    route = []
    for low in range(count):
        high = low | 1 << distance
        if high != low and high < count:
            route += [(low, high), (high, low)]
    return lax.ppermute(block, axis, route)


def shards_any(
    interface_stiffness,
    lower_factor,
    upper_factor,
    modes,
    gyro_rows,
    gyro_coupling,
    spin_softening,
    speed_index,
):
    tile_count = lax.axis_size("tile")
    branch_count = lax.axis_size("subtree")
    tile_pos = lax.axis_index("tile")
    branch_pos = lax.axis_index("subtree")
    mode_count = modes.shape[1]
    mode_cols = mode_count // branch_count
    mode_rows_dev = mode_count // tile_count
    coupled = jnp.einsum(
        "lrk,lkn->rn",
        lower_factor,
        lax.all_gather(upper_factor, "tile", axis=2, tiled=True),
        preferred_element_type=jnp.float32,
    )
    schur_part = jnp.sum(interface_stiffness, axis=0) - coupled
    own_width = schur_part.shape[1] // branch_count
    for level_bit in range(branch_count.bit_length() - 1):
        schur_part = schur_part + partner(schur_part, "subtree", level_bit)
    schur_out = lax.dynamic_slice_in_dim(schur_part, branch_pos * own_width, own_width, 1)
    segment = lax.all_gather(modes, "tile", axis=0, tiled=True)
    wanted = lax.dynamic_slice_in_dim(segment, branch_pos * mode_cols, mode_cols, 1)
    response = jnp.dot(
        schur_part,
        wanted.astype(jnp.float32),
        precision=lax.Precision.HIGHEST,
        preferred_element_type=jnp.float32,
    )
    partial_value = jnp.einsum(
        "rm,rc->mc",
        modes.astype(jnp.float32),
        response,
        precision=lax.Precision.HIGHEST,
        preferred_element_type=jnp.float32,
    )
    stiff_block = lax.psum_scatter(partial_value, "tile", scatter_dimension=0, tiled=True)
    picked = jnp.take(segment, gyro_rows, axis=0, mode="clip").astype(jnp.float32)
    gyro_block, spin_block = gyro_parts(
        picked,
        gyro_coupling,
        spin_softening,
        tile_pos * mode_rows_dev,
        mode_rows_dev,
        branch_pos * mode_cols,
        mode_cols,
    )
    return (schur_out, combine(stiff_block, gyro_block, spin_block, speed_index))


def gray(i):
    return i ^ (i >> 1)


def ring_z(place, k):
    return gray((gray(place[0] >> 1) + (4 - k)) & 3)


def block_at(place, j, k):
    return ring_z(place, k) * 2 + ((place[0] & 1) ^ j)


def keeps(place, k):
    return (ring_z(place, k) & 1) == (place[1] & 1)


def stays(place):
    return ((gray(place[0] >> 1) - gray(place[1])) & 1) == 0


IN_VMEM = pl.BlockSpec(memory_space=pltpu.VMEM)


def call(body, operands, outs, scratch=()):
    return pl.pallas_call(
        body,
        out_shape=[jax.ShapeDtypeStruct(shape, dtype) for shape, dtype in outs],
        in_specs=[pl.BlockSpec(memory_space=pltpu.SMEM)] + [IN_VMEM] * (len(operands) - 1),
        out_specs=[IN_VMEM] * len(outs),
        scratch_shapes=scratch,
        compiler_params=pltpu.CompilerParams(vmem_limit_bytes=GRANT),
        cost_estimate=pl.CostEstimate(flops=1 << 20, bytes_accessed=1 << 18, transcendentals=0),
    )(*operands)


def mul(left, right):
    return jnp.dot(left, right, preferred_element_type=jnp.float32)


def mul_wide(left, right):
    high = left.astype(jnp.bfloat16)
    low = (left - high.astype(jnp.float32)).astype(jnp.bfloat16)
    return mul(high, right) + mul(low, right)


ROW_STEPS = 4


def shares(place, stiffness, lower, blocks):
    rows = stiffness.shape[0]
    depth = lower.shape[1]
    cols = blocks[0][2][0].shape[1]
    step = rows // ROW_STEPS
    operands = [place, stiffness, lower]
    outs = []
    for _, _, pieces, old in blocks:
        operands += list(pieces) + ([] if old is None else [old])
        outs += [((rows, cols), jnp.float32)] * (1 if old is None else 2)

    def body(at, stiff, low, *refs):
        sources, targets = list(refs[: len(operands) - 3]), list(refs[len(operands) - 3 :])
        for j, k, pieces, old in blocks:
            uppers = [sources.pop(0) for _ in pieces]
            before = None if old is None else sources.pop(0)
            wanted = [targets.pop(0) for _ in range(1 if old is None else 2)]
            first_col = pl.multiple_of(block_at(at, j, k) * cols, cols)
            size = depth // len(pieces)

            @pl.loop(0, ROW_STEPS)
            def _(i):
                part = pl.ds(pl.multiple_of(i * step, step), step)
                value = stiff[part, pl.ds(first_col, cols)]
                for n, ref in enumerate(uppers):
                    value -= mul(low[part, n * size : (n + 1) * size], ref[:size, :])
                if before is None:
                    wanted[0][part, :] = value
                else:
                    sent, kept = wanted
                    keep_old = keeps(at, k - 2)
                    past = before[part, :]
                    sent[part, :] = jnp.where(keep_old, value, past)
                    kept[part, :] = jnp.where(keep_old, past, value)

    return call(body, operands, outs)


def fill_modes(at, target, near, beside, n):
    half, width = near.shape[1], target.shape[1]
    for other, source in enumerate((near, beside)):
        first = pl.multiple_of(((at[1] & 1) ^ other) * 2 * half, 2 * half)
        target[pl.ds(first, half), :] = source[n, :, :width]
        target[pl.ds(first + half, half), :] = source[n, :, width:]


def respond(place, groups, pairs, start, rows, mode_count):
    cols = pairs[0][3].shape[1]
    flat = [g for pair in groups for g in pair]
    shares_in = [s for p in pairs for s in p[3:]]
    plus = [] if start is None else [start]
    step = rows // ROW_STEPS

    def body(at, *refs):
        group_refs = refs[: len(flat)]
        share_refs = refs[len(flat) : len(flat) + len(shares_in)]
        out, scratch = refs[-2], refs[-1]
        for m, (older, newer, k, _, _) in enumerate(pairs):
            keep_old = keeps(at, k)

            def fill(slot, which):
                group, n = which
                fill_modes(at, scratch.at[slot], group_refs[2 * group], group_refs[2 * group + 1], n)

            @pl.when(keep_old)
            def _():
                fill(2 * m, newer)
                fill(2 * m + 1, older)

            @pl.when(jnp.logical_not(keep_old))
            def _():
                fill(2 * m, older)
                fill(2 * m + 1, newer)

        @pl.loop(0, ROW_STEPS)
        def _(i):
            part = pl.ds(pl.multiple_of(i * step, step), step)
            if plus:
                total = refs[len(flat) + len(shares_in)][part, :]
            else:
                total = jnp.zeros((step, mode_count), jnp.float32)
            for n in range(len(shares_in)):
                total += mul_wide(share_refs[n][part, :], scratch[n])
            out[part, :] = total

    return call(
        body,
        [place] + flat + shares_in + plus,
        [((rows, mode_count), jnp.float32)],
        [pltpu.VMEM((len(shares_in), cols, mode_count), jnp.bfloat16)],
    )[0]


def reduce_modes(place, groups, pair, response, modes, branches, tiles):
    mode_count = modes.shape[1]
    group = mode_count // tiles // 2
    older, newer, k, sent, kept = pair
    rows, cols = sent.shape
    flat = [g for both in groups for g in both]

    def body(at, *refs):
        group_refs = refs[: len(flat)]
        sent_ref, kept_ref, resp, mode, pieces, scratch = refs[len(flat) :]
        keep_old = keeps(at, k)

        def fill(slot, which):
            fill_modes(
                at, scratch.at[slot], group_refs[2 * which[0]], group_refs[2 * which[0] + 1], which[1]
            )

        @pl.when(keep_old)
        def _():
            fill(0, newer)
            fill(1, older)

        @pl.when(jnp.logical_not(keep_old))
        def _():
            fill(0, older)
            fill(1, newer)

        total = resp[...] + mul_wide(sent_ref[...], scratch[0]) + mul_wide(kept_ref[...], scratch[1])
        high = total.astype(jnp.bfloat16)
        rest = (total - high.astype(jnp.float32)).astype(jnp.bfloat16)
        across = (((0,), (0,)), ((), ()))
        reduced = lax.dot_general(
            mode[...], high, across, preferred_element_type=jnp.float32
        ) + lax.dot_general(mode[...], rest, across, preferred_element_type=jnp.float32)
        split = reduced.reshape(tiles, 2, group, mode_count)
        upper = split[:, 0].reshape(tiles * group, mode_count)
        under = split[:, 1].reshape(tiles * group, mode_count)
        left = lax.broadcasted_iota(jnp.int32, (tiles * group, 128), 1) < 64
        for half in range(branches // 2):
            u = upper[:, 128 * half : 128 * half + 128]
            v = under[:, 128 * half : 128 * half + 128]
            pieces[2 * half] = jnp.where(left, u, pltpu.roll(v, 64, 1))
            pieces[2 * half + 1] = jnp.where(left, pltpu.roll(u, 64, 1), v)

    return call(
        body,
        [place] + flat + [sent, kept, response, modes],
        [((branches, tiles * group, 128), jnp.float32)],
        [pltpu.VMEM((2, cols, mode_count), jnp.bfloat16)],
    )[0]


def pick(which, arrays):
    value = arrays[-1]
    for n in range(len(arrays) - 2, -1, -1):
        value = jnp.where(which == n, arrays[n], value)
    return value


def to_wire(value):
    return (value * SHARE_SCALE).astype(jnp.float16)


def from_wire(value):
    return value.astype(jnp.float32) * (1.0 / SHARE_SCALE)


def shards_ring(
    interface_stiffness,
    lower_factor,
    upper_factor,
    modes,
    gyro_rows,
    gyro_coupling,
    spin_softening,
    speed_index,
):
    f32 = jnp.float32
    tiles = lax.axis_size("tile")
    branches = lax.axis_size("subtree")
    tile = lax.axis_index("tile")
    branch = lax.axis_index("subtree")
    place = jnp.stack([tile, branch]).astype(jnp.int32)
    stiffness = interface_stiffness[0]
    lower = lower_factor[0]
    upper = upper_factor[0]
    rows = stiffness.shape[0]
    depth, cols = upper.shape
    mode_count = modes.shape[1]

    def ring_pairs(turn):
        return [
            (gray(p) * 2 + a, gray((p + 1) % 4) * 2 + a)
            if turn
            else (gray((p + 1) % 4) * 2 + 1 - a, gray(p) * 2 + a)
            for p in range(4)
            for a in range(2)
        ]

    def over_z(block):
        return lax.ppermute(block, "tile", ring_pairs(True))

    def over_x(block):
        return lax.ppermute(block, "tile", [(i, i ^ 1) for i in range(tiles)])

    def over_y(block):
        return lax.ppermute(block, "subtree", [(i, i ^ 2) for i in range(branches)])

    def over_core(block):
        return lax.ppermute(block, "subtree", [(i, i ^ 1) for i in range(branches)])

    def over_y_of(block, first):
        route = [
            (b * tiles + t, (b ^ 2) * tiles + t)
            for b in range(branches)
            for t in range(tiles)
            if stays((t, b)) != first
        ]
        return lax.ppermute(block, ("subtree", "tile"), route)

    chunk = modes.shape[0] // 2
    mine = lax.dynamic_slice_in_dim(modes, (branch & 1) * chunk, chunk, 0)
    mine = jnp.concatenate([mine[: chunk // 2], mine[chunk // 2 :]], axis=1)
    load = jnp.concatenate([upper, mine], axis=0)
    mode_far = lax.ppermute(mine, "tile", ring_pairs(False))
    z1, x0 = lax.optimization_barrier((over_z(load), over_x(load)))
    z2, x1 = lax.optimization_barrier((over_z(z1), over_x(z1)))
    z3, x2 = lax.optimization_barrier((over_z(z2), over_x(z2)))
    cut = depth // 2
    x3_low, x3_high = over_x(z3[:cut]), over_z(x2[cut:depth])

    def spread(pieces):
        near = jnp.stack(pieces)
        return near, over_core(near)

    early = spread([mine, z1[depth:], x0[depth:], mode_far])
    middle = spread([z2[depth:], x1[depth:]])
    late = spread([z3[depth:], x2[depth:]])
    early_n, middle_n, late_n = 0, 1, 2
    groups = [early, middle, late]

    (p00,) = shares(place, stiffness, lower, [(0, 0, [load], None)])
    p01, p10 = shares(place, stiffness, lower, [(0, 1, [z1], None), (1, 0, [x0], None)])
    sent_a0, kept_a0, p11 = shares(
        place, stiffness, lower, [(0, 2, [z2], p00), (1, 1, [x1], None)]
    )
    sent_b0, kept_b0, sent_a1, kept_a1 = shares(
        place, stiffness, lower, [(0, 3, [z3], p01), (1, 2, [x2], p10)]
    )
    chip_a0 = kept_a0 + over_core(sent_a0)
    came_a0 = over_y_of(to_wire(chip_a0), True)
    chip_b0 = kept_b0 + over_core(sent_b0)
    wire_b0 = to_wire(chip_b0)
    came_b0 = over_y_of(wire_b0, False)
    chip_a1 = kept_a1 + over_core(sent_a1)
    wire_a1 = to_wire(chip_a1)
    came_a1 = over_y_of(wire_a1, True)

    pair_a0 = ((early_n, 0), (middle_n, 0), 0, sent_a0, kept_a0)
    pair_b0 = ((early_n, 1), (late_n, 0), 1, sent_b0, kept_b0)
    pair_a1 = ((early_n, 2), (late_n, 1), 0, sent_a1, kept_a1)
    response = respond(place, [early, middle], [pair_a0], None, rows, mode_count)
    response = respond(place, groups, [pair_b0, pair_a1], response, rows, mode_count)
    x3_low, x3_high, came_a0, _, _ = lax.optimization_barrier(
        (x3_low, x3_high, came_a0, wire_b0, wire_a1)
    )
    sent_b1, kept_b1 = shares(place, stiffness, lower, [(1, 3, [x3_low, x3_high], p11)])

    mode_rows = mode_count // tiles
    mode_cols = mode_count // branches
    pair_b1 = ((0, 0), (0, 1), 1, sent_b1, kept_b1)
    last_two = (
        jnp.stack([middle[0][1], early[0][3]]),
        jnp.stack([middle[1][1], early[1][3]]),
    )
    pieces = reduce_modes(place, [last_two], pair_b1, response, modes, branches, tiles)
    pieces = pieces.reshape(branches * tiles, mode_rows // 2, 2 * mode_cols)
    pieces, gyro_rows = lax.optimization_barrier((pieces, gyro_rows))
    summed = jnp.sum(lax.all_to_all(pieces, ("subtree", "tile"), 0, 0), axis=0)
    stiff_block = jnp.concatenate([summed[:, :mode_cols], summed[:, mode_cols:]], axis=0)

    chip_b1 = kept_b1 + over_core(sent_b1)
    wire_b1, came_a1, came_b0 = lax.optimization_barrier((to_wire(chip_b1), came_a1, came_b0))
    came_b1 = over_y_of(wire_b1, False)
    here = stays((tile, branch))
    left = tile & 1
    first = jnp.where(here, chip_a0 + from_wire(came_a0), chip_b0 + from_wire(came_b0))
    ready = jnp.concatenate([first, first], axis=1)
    second = jnp.where(here, chip_a1 + from_wire(came_a1), chip_b1 + from_wire(came_b1))
    schur_out = lax.dynamic_update_slice_in_dim(ready, second, (1 - left) * cols, 1)

    row_tile, row_in = gyro_rows // modes.shape[0], gyro_rows % modes.shape[0]
    turn = (gray(tile // 2) - gray(row_tile // 2)) & 3
    index = ((row_tile ^ tile) & 1) * 4 + turn
    block = pick(index, [0, 1, 4, 6, 2, 5, 7, 3])
    half_row = row_in % chunk
    table = jnp.concatenate([g[side] for side in range(2) for g in groups]).reshape(
        -1, 2 * mode_count
    )
    line = (((row_in // chunk) ^ branch) & 1) * 8 + block
    wide = jnp.take(
        table, line * (chunk // 2) + half_row % (chunk // 2), axis=0, mode="clip"
    )
    picked = jnp.where(
        (half_row < chunk // 2)[:, None], wide[:, :mode_count], wide[:, mode_count:]
    ).astype(f32)
    gyro_block, spin_block = gyro_parts(
        picked,
        gyro_coupling,
        spin_softening,
        tile * mode_rows,
        mode_rows,
        branch * mode_cols,
        mode_cols,
    )
    return (schur_out, combine(stiff_block, gyro_block, spin_block, speed_index))


def solution(mesh):
    placed = (
        P("subtree", "tile", None),
        P("subtree", "tile", None),
        P("subtree", None, "tile"),
        P("tile", None),
        P(),
        P(),
        P(),
        P(),
    )
    ring = (mesh.shape["subtree"], mesh.shape["tile"]) == (4, 8)
    return jax.shard_map(
        shards_ring if ring else shards_any,
        mesh=mesh,
        in_specs=placed,
        out_specs=(P("tile", "subtree"), P(None, "tile", "subtree")),
        check_vma=False,
    )
```

```python
import jax
import jax.numpy as jnp
from jax import lax
from jax.experimental import pallas as pl
from jax.experimental.pallas import tpu as pltpu
from jax.sharding import PartitionSpec as P

SPEED_STEPS = 64


OMEGA_TOP = 2.0

SHARE_SCALE = 32.0

GRANT = 16 << 20


def omegas(speed_index):
    return OMEGA_TOP * (speed_index.astype(jnp.float32) + 1.0) / SPEED_STEPS


def combine(stiff_block, gyro_block, spin_block, speed_index):
    speeds_omega = omegas(speed_index)
    return (
        stiff_block[None]
        + speeds_omega[:, None, None] * gyro_block[None]
        - (speeds_omega * speeds_omega)[:, None, None] * spin_block[None]
    )


def gyro_parts(picked, gyro_coupling, spin_softening, left_first, left_count, right_first, right_count):
    skew_part = 0.5 * (gyro_coupling - gyro_coupling.T)
    left_modes = lax.dynamic_slice_in_dim(picked, left_first, left_count, 1)
    right_modes = lax.dynamic_slice_in_dim(picked, right_first, right_count, 1)
    turned = jnp.dot(
        skew_part, right_modes, precision=lax.Precision.HIGHEST, preferred_element_type=jnp.float32
    )
    gyro_block = jnp.einsum(
        "gm,gc->mc",
        left_modes,
        turned,
        precision=lax.Precision.HIGHEST,
        preferred_element_type=jnp.float32,
    )
    spin_block = jnp.einsum(
        "gm,gc->mc",
        left_modes,
        spin_softening[:, None] * right_modes,
        precision=lax.Precision.HIGHEST,
        preferred_element_type=jnp.float32,
    )
    return gyro_block, spin_block


def partner(block, axis, distance):
    count = lax.axis_size(axis)
    route = []
    for low in range(count):
        high = low | 1 << distance
        if high != low and high < count:
            route += [(low, high), (high, low)]
    return lax.ppermute(block, axis, route)


def shards_any(
    interface_stiffness,
    lower_factor,
    upper_factor,
    modes,
    gyro_rows,
    gyro_coupling,
    spin_softening,
    speed_index,
):
    tile_count = lax.axis_size("tile")
    branch_count = lax.axis_size("subtree")
    tile_pos = lax.axis_index("tile")
    branch_pos = lax.axis_index("subtree")
    mode_count = modes.shape[1]
    mode_cols = mode_count // branch_count
    mode_rows_dev = mode_count // tile_count
    coupled = jnp.einsum(
        "lrk,lkn->rn",
        lower_factor,
        lax.all_gather(upper_factor, "tile", axis=2, tiled=True),
        preferred_element_type=jnp.float32,
    )
    schur_part = jnp.sum(interface_stiffness, axis=0) - coupled
    own_width = schur_part.shape[1] // branch_count
    for level_bit in range(branch_count.bit_length() - 1):
        schur_part = schur_part + partner(schur_part, "subtree", level_bit)
    schur_out = lax.dynamic_slice_in_dim(schur_part, branch_pos * own_width, own_width, 1)
    segment = lax.all_gather(modes, "tile", axis=0, tiled=True)
    wanted = lax.dynamic_slice_in_dim(segment, branch_pos * mode_cols, mode_cols, 1)
    response = jnp.dot(
        schur_part,
        wanted.astype(jnp.float32),
        precision=lax.Precision.HIGHEST,
        preferred_element_type=jnp.float32,
    )
    partial_value = jnp.einsum(
        "rm,rc->mc",
        modes.astype(jnp.float32),
        response,
        precision=lax.Precision.HIGHEST,
        preferred_element_type=jnp.float32,
    )
    stiff_block = lax.psum_scatter(partial_value, "tile", scatter_dimension=0, tiled=True)
    picked = jnp.take(segment, gyro_rows, axis=0, mode="clip").astype(jnp.float32)
    gyro_block, spin_block = gyro_parts(
        picked,
        gyro_coupling,
        spin_softening,
        tile_pos * mode_rows_dev,
        mode_rows_dev,
        branch_pos * mode_cols,
        mode_cols,
    )
    return (schur_out, combine(stiff_block, gyro_block, spin_block, speed_index))


def gray(i):
    return i ^ (i >> 1)


def ring_z(place, k):
    return gray((gray(place[0] >> 1) + (4 - k)) & 3)


def block_at(place, j, k):
    return ring_z(place, k) * 2 + ((place[0] & 1) ^ j)


def keeps(place, k):
    return (ring_z(place, k) & 1) == (place[1] & 1)


def stays(place):
    return ((gray(place[0] >> 1) - gray(place[1])) & 1) == 0


IN_VMEM = pl.BlockSpec(memory_space=pltpu.VMEM)


def call(body, operands, outs, scratch=()):
    return pl.pallas_call(
        body,
        out_shape=[jax.ShapeDtypeStruct(shape, dtype) for shape, dtype in outs],
        in_specs=[pl.BlockSpec(memory_space=pltpu.SMEM)] + [IN_VMEM] * (len(operands) - 1),
        out_specs=[IN_VMEM] * len(outs),
        scratch_shapes=scratch,
        compiler_params=pltpu.CompilerParams(vmem_limit_bytes=GRANT),
        cost_estimate=pl.CostEstimate(flops=1 << 31, bytes_accessed=1 << 20, transcendentals=0),
    )(*operands)


def mul(left, right):
    return jnp.dot(left, right, preferred_element_type=jnp.float32)


def mul_wide(left, right):
    high = left.astype(jnp.bfloat16)
    low = (left - high.astype(jnp.float32)).astype(jnp.bfloat16)
    return mul(high, right) + mul(low, right)


ROW_STEPS = 4


def shares(place, stiffness, lower, blocks):
    rows = stiffness.shape[0]
    depth = lower.shape[1]
    cols = blocks[0][2][0].shape[1]
    step = rows // ROW_STEPS
    operands = [place, stiffness, lower]
    outs = []
    for _, _, pieces, old in blocks:
        operands += list(pieces) + ([] if old is None else [old])
        outs += [((rows, cols), jnp.float32)] * (1 if old is None else 2)

    def body(at, stiff, low, *refs):
        sources, targets = list(refs[: len(operands) - 3]), list(refs[len(operands) - 3 :])
        for j, k, pieces, old in blocks:
            uppers = [sources.pop(0) for _ in pieces]
            before = None if old is None else sources.pop(0)
            wanted = [targets.pop(0) for _ in range(1 if old is None else 2)]
            first_col = pl.multiple_of(block_at(at, j, k) * cols, cols)
            size = depth // len(pieces)

            @pl.loop(0, ROW_STEPS)
            def _(i):
                part = pl.ds(pl.multiple_of(i * step, step), step)
                value = stiff[part, pl.ds(first_col, cols)]
                for n, ref in enumerate(uppers):
                    value -= mul(low[part, n * size : (n + 1) * size], ref[:size, :])
                if before is None:
                    wanted[0][part, :] = value
                else:
                    sent, kept = wanted
                    keep_old = keeps(at, k - 2)
                    past = before[part, :]
                    sent[part, :] = jnp.where(keep_old, value, past)
                    kept[part, :] = jnp.where(keep_old, past, value)

    return call(body, operands, outs)


def fill_modes(at, target, near, beside, n):
    half, width = near.shape[1], target.shape[1]
    for other, source in enumerate((near, beside)):
        first = pl.multiple_of(((at[1] & 1) ^ other) * 2 * half, 2 * half)
        target[pl.ds(first, half), :] = source[n, :, :width]
        target[pl.ds(first + half, half), :] = source[n, :, width:]


def respond(place, groups, pairs, start, rows, mode_count):
    cols = pairs[0][3].shape[1]
    flat = [g for pair in groups for g in pair]
    shares_in = [s for p in pairs for s in p[3:]]
    plus = [] if start is None else [start]
    step = rows // ROW_STEPS

    def body(at, *refs):
        group_refs = refs[: len(flat)]
        share_refs = refs[len(flat) : len(flat) + len(shares_in)]
        out, scratch = refs[-2], refs[-1]
        for m, (older, newer, k, _, _) in enumerate(pairs):
            keep_old = keeps(at, k)

            def fill(slot, which):
                group, n = which
                fill_modes(at, scratch.at[slot], group_refs[2 * group], group_refs[2 * group + 1], n)

            @pl.when(keep_old)
            def _():
                fill(2 * m, newer)
                fill(2 * m + 1, older)

            @pl.when(jnp.logical_not(keep_old))
            def _():
                fill(2 * m, older)
                fill(2 * m + 1, newer)

        @pl.loop(0, ROW_STEPS)
        def _(i):
            part = pl.ds(pl.multiple_of(i * step, step), step)
            if plus:
                total = refs[len(flat) + len(shares_in)][part, :]
            else:
                total = jnp.zeros((step, mode_count), jnp.float32)
            for n in range(len(shares_in)):
                total += mul_wide(share_refs[n][part, :], scratch[n])
            out[part, :] = total

    return call(
        body,
        [place] + flat + shares_in + plus,
        [((rows, mode_count), jnp.float32)],
        [pltpu.VMEM((len(shares_in), cols, mode_count), jnp.bfloat16)],
    )[0]


def reduce_modes(place, groups, pair, response, modes, branches, tiles):
    mode_count = modes.shape[1]
    group = mode_count // tiles // 2
    older, newer, k, sent, kept = pair
    rows, cols = sent.shape
    flat = [g for both in groups for g in both]

    def body(at, *refs):
        group_refs = refs[: len(flat)]
        sent_ref, kept_ref, resp, mode, pieces, scratch = refs[len(flat) :]
        keep_old = keeps(at, k)

        def fill(slot, which):
            fill_modes(
                at, scratch.at[slot], group_refs[2 * which[0]], group_refs[2 * which[0] + 1], which[1]
            )

        @pl.when(keep_old)
        def _():
            fill(0, newer)
            fill(1, older)

        @pl.when(jnp.logical_not(keep_old))
        def _():
            fill(0, older)
            fill(1, newer)

        total = resp[...] + mul_wide(sent_ref[...], scratch[0]) + mul_wide(kept_ref[...], scratch[1])
        high = total.astype(jnp.bfloat16)
        rest = (total - high.astype(jnp.float32)).astype(jnp.bfloat16)
        across = (((0,), (0,)), ((), ()))
        reduced = lax.dot_general(
            mode[...], high, across, preferred_element_type=jnp.float32
        ) + lax.dot_general(mode[...], rest, across, preferred_element_type=jnp.float32)
        split = reduced.reshape(tiles, 2, group, mode_count)
        upper = split[:, 0].reshape(tiles * group, mode_count)
        under = split[:, 1].reshape(tiles * group, mode_count)
        left = lax.broadcasted_iota(jnp.int32, (tiles * group, 128), 1) < 64
        for half in range(branches // 2):
            u = upper[:, 128 * half : 128 * half + 128]
            v = under[:, 128 * half : 128 * half + 128]
            pieces[2 * half] = jnp.where(left, u, pltpu.roll(v, 64, 1))
            pieces[2 * half + 1] = jnp.where(left, pltpu.roll(u, 64, 1), v)

    return call(
        body,
        [place] + flat + [sent, kept, response, modes],
        [((branches, tiles * group, 128), jnp.float32)],
        [pltpu.VMEM((2, cols, mode_count), jnp.bfloat16)],
    )[0]


def pick(which, arrays):
    value = arrays[-1]
    for n in range(len(arrays) - 2, -1, -1):
        value = jnp.where(which == n, arrays[n], value)
    return value


def to_wire(value):
    return (value * SHARE_SCALE).astype(jnp.float16)


def from_wire(value):
    return value.astype(jnp.float32) * (1.0 / SHARE_SCALE)


def shards_ring(
    interface_stiffness,
    lower_factor,
    upper_factor,
    modes,
    gyro_rows,
    gyro_coupling,
    spin_softening,
    speed_index,
):
    f32 = jnp.float32
    tiles = lax.axis_size("tile")
    branches = lax.axis_size("subtree")
    tile = lax.axis_index("tile")
    branch = lax.axis_index("subtree")
    place = jnp.stack([tile, branch]).astype(jnp.int32)
    stiffness = interface_stiffness[0]
    lower = lower_factor[0]
    upper = upper_factor[0]
    rows = stiffness.shape[0]
    depth, cols = upper.shape
    mode_count = modes.shape[1]

    def ring_pairs(turn):
        return [
            (gray(p) * 2 + a, gray((p + 1) % 4) * 2 + a)
            if turn
            else (gray((p + 1) % 4) * 2 + 1 - a, gray(p) * 2 + a)
            for p in range(4)
            for a in range(2)
        ]

    def over_z(block):
        return lax.ppermute(block, "tile", ring_pairs(True))

    def over_x(block):
        return lax.ppermute(block, "tile", [(i, i ^ 1) for i in range(tiles)])

    def over_y(block):
        return lax.ppermute(block, "subtree", [(i, i ^ 2) for i in range(branches)])

    def over_core(block):
        return lax.ppermute(block, "subtree", [(i, i ^ 1) for i in range(branches)])

    def over_y_of(block, first):
        route = [
            (b * tiles + t, (b ^ 2) * tiles + t)
            for b in range(branches)
            for t in range(tiles)
            if stays((t, b)) != first
        ]
        return lax.ppermute(block, ("subtree", "tile"), route)

    chunk = modes.shape[0] // 2
    mine = lax.dynamic_slice_in_dim(modes, (branch & 1) * chunk, chunk, 0)
    mine = jnp.concatenate([mine[: chunk // 2], mine[chunk // 2 :]], axis=1)
    load = jnp.concatenate([upper, mine], axis=0)
    mode_far = lax.ppermute(mine, "tile", ring_pairs(False))
    z1, x0 = lax.optimization_barrier((over_z(load), over_x(load)))
    z2, x1 = lax.optimization_barrier((over_z(z1), over_x(z1)))
    z3, x2 = lax.optimization_barrier((over_z(z2), over_x(z2)))
    cut = depth // 2
    x3_low, x3_high = over_x(z3[:cut]), over_z(x2[cut:depth])

    def spread(pieces):
        near = jnp.stack(pieces)
        return near, over_core(near)

    early = spread([mine, z1[depth:], x0[depth:], mode_far])
    middle = spread([z2[depth:], x1[depth:]])
    late = spread([z3[depth:], x2[depth:]])
    early_n, middle_n, late_n = 0, 1, 2
    groups = [early, middle, late]

    (p00,) = shares(place, stiffness, lower, [(0, 0, [load], None)])
    p01, p10 = shares(place, stiffness, lower, [(0, 1, [z1], None), (1, 0, [x0], None)])
    sent_a0, kept_a0, p11 = shares(
        place, stiffness, lower, [(0, 2, [z2], p00), (1, 1, [x1], None)]
    )
    sent_b0, kept_b0, sent_a1, kept_a1 = shares(
        place, stiffness, lower, [(0, 3, [z3], p01), (1, 2, [x2], p10)]
    )
    chip_a0 = kept_a0 + over_core(sent_a0)
    came_a0 = over_y_of(to_wire(chip_a0), True)
    chip_b0 = kept_b0 + over_core(sent_b0)
    wire_b0 = to_wire(chip_b0)
    came_b0 = over_y_of(wire_b0, False)
    chip_a1 = kept_a1 + over_core(sent_a1)
    wire_a1 = to_wire(chip_a1)
    came_a1 = over_y_of(wire_a1, True)

    pair_a0 = ((early_n, 0), (middle_n, 0), 0, sent_a0, kept_a0)
    pair_b0 = ((early_n, 1), (late_n, 0), 1, sent_b0, kept_b0)
    pair_a1 = ((early_n, 2), (late_n, 1), 0, sent_a1, kept_a1)
    response = respond(place, [early, middle], [pair_a0], None, rows, mode_count)
    response = respond(place, groups, [pair_b0, pair_a1], response, rows, mode_count)
    x3_low, x3_high, came_a0, _, _ = lax.optimization_barrier(
        (x3_low, x3_high, came_a0, wire_b0, wire_a1)
    )
    sent_b1, kept_b1 = shares(place, stiffness, lower, [(1, 3, [x3_low, x3_high], p11)])

    mode_rows = mode_count // tiles
    mode_cols = mode_count // branches
    pair_b1 = ((0, 0), (0, 1), 1, sent_b1, kept_b1)
    last_two = (
        jnp.stack([middle[0][1], early[0][3]]),
        jnp.stack([middle[1][1], early[1][3]]),
    )
    pieces = reduce_modes(place, [last_two], pair_b1, response, modes, branches, tiles)
    pieces = pieces.reshape(branches * tiles, mode_rows // 2, 2 * mode_cols)
    pieces, gyro_rows = lax.optimization_barrier((pieces, gyro_rows))
    summed = jnp.sum(lax.all_to_all(pieces, ("subtree", "tile"), 0, 0), axis=0)
    stiff_block = jnp.concatenate([summed[:, :mode_cols], summed[:, mode_cols:]], axis=0)

    chip_b1 = kept_b1 + over_core(sent_b1)
    wire_b1, came_a1, came_b0 = lax.optimization_barrier((to_wire(chip_b1), came_a1, came_b0))
    came_b1 = over_y_of(wire_b1, False)
    here = stays((tile, branch))
    left = tile & 1
    first = jnp.where(here, chip_a0 + from_wire(came_a0), chip_b0 + from_wire(came_b0))
    ready = jnp.concatenate([first, first], axis=1)
    second = jnp.where(here, chip_a1 + from_wire(came_a1), chip_b1 + from_wire(came_b1))
    schur_out = lax.dynamic_update_slice_in_dim(ready, second, (1 - left) * cols, 1)

    row_tile, row_in = gyro_rows // modes.shape[0], gyro_rows % modes.shape[0]
    turn = (gray(tile // 2) - gray(row_tile // 2)) & 3
    index = ((row_tile ^ tile) & 1) * 4 + turn
    block = pick(index, [0, 1, 4, 6, 2, 5, 7, 3])
    half_row = row_in % chunk
    table = jnp.concatenate([g[side] for side in range(2) for g in groups]).reshape(
        -1, 2 * mode_count
    )
    line = (((row_in // chunk) ^ branch) & 1) * 8 + block
    wide = jnp.take(
        table, line * (chunk // 2) + half_row % (chunk // 2), axis=0, mode="clip"
    )
    picked = jnp.where(
        (half_row < chunk // 2)[:, None], wide[:, :mode_count], wide[:, mode_count:]
    ).astype(f32)
    gyro_block, spin_block = gyro_parts(
        picked,
        gyro_coupling,
        spin_softening,
        tile * mode_rows,
        mode_rows,
        branch * mode_cols,
        mode_cols,
    )
    return (schur_out, combine(stiff_block, gyro_block, spin_block, speed_index))


def solution(mesh):
    placed = (
        P("subtree", "tile", None),
        P("subtree", "tile", None),
        P("subtree", None, "tile"),
        P("tile", None),
        P(),
        P(),
        P(),
        P(),
    )
    ring = (mesh.shape["subtree"], mesh.shape["tile"]) == (4, 8)
    return jax.shard_map(
        shards_ring if ring else shards_any,
        mesh=mesh,
        in_specs=placed,
        out_specs=(P("tile", "subtree"), P(None, "tile", "subtree")),
        check_vma=False,
    )
```

```python
import jax
import jax.numpy as jnp
from jax import lax
from jax.experimental import pallas as pl
from jax.experimental.pallas import tpu as pltpu
from jax.sharding import PartitionSpec as P

SPEED_STEPS = 64


OMEGA_TOP = 2.0

SHARE_SCALE = 32.0

GRANT = 16 << 20


def omegas(speed_index):
    return OMEGA_TOP * (speed_index.astype(jnp.float32) + 1.0) / SPEED_STEPS


def combine(stiff_block, gyro_block, spin_block, speed_index):
    speeds_omega = omegas(speed_index)
    return (
        stiff_block[None]
        + speeds_omega[:, None, None] * gyro_block[None]
        - (speeds_omega * speeds_omega)[:, None, None] * spin_block[None]
    )


def gyro_parts(picked, gyro_coupling, spin_softening, left_first, left_count, right_first, right_count):
    skew_part = 0.5 * (gyro_coupling - gyro_coupling.T)
    left_modes = lax.dynamic_slice_in_dim(picked, left_first, left_count, 1)
    right_modes = lax.dynamic_slice_in_dim(picked, right_first, right_count, 1)
    turned = jnp.dot(
        skew_part, right_modes, precision=lax.Precision.HIGHEST, preferred_element_type=jnp.float32
    )
    gyro_block = jnp.einsum(
        "gm,gc->mc",
        left_modes,
        turned,
        precision=lax.Precision.HIGHEST,
        preferred_element_type=jnp.float32,
    )
    spin_block = jnp.einsum(
        "gm,gc->mc",
        left_modes,
        spin_softening[:, None] * right_modes,
        precision=lax.Precision.HIGHEST,
        preferred_element_type=jnp.float32,
    )
    return gyro_block, spin_block


def partner(block, axis, distance):
    count = lax.axis_size(axis)
    route = []
    for low in range(count):
        high = low | 1 << distance
        if high != low and high < count:
            route += [(low, high), (high, low)]
    return lax.ppermute(block, axis, route)


def shards_any(
    interface_stiffness,
    lower_factor,
    upper_factor,
    modes,
    gyro_rows,
    gyro_coupling,
    spin_softening,
    speed_index,
):
    tile_count = lax.axis_size("tile")
    branch_count = lax.axis_size("subtree")
    tile_pos = lax.axis_index("tile")
    branch_pos = lax.axis_index("subtree")
    mode_count = modes.shape[1]
    mode_cols = mode_count // branch_count
    mode_rows_dev = mode_count // tile_count
    coupled = jnp.einsum(
        "lrk,lkn->rn",
        lower_factor,
        lax.all_gather(upper_factor, "tile", axis=2, tiled=True),
        preferred_element_type=jnp.float32,
    )
    schur_part = jnp.sum(interface_stiffness, axis=0) - coupled
    own_width = schur_part.shape[1] // branch_count
    for level_bit in range(branch_count.bit_length() - 1):
        schur_part = schur_part + partner(schur_part, "subtree", level_bit)
    schur_out = lax.dynamic_slice_in_dim(schur_part, branch_pos * own_width, own_width, 1)
    segment = lax.all_gather(modes, "tile", axis=0, tiled=True)
    wanted = lax.dynamic_slice_in_dim(segment, branch_pos * mode_cols, mode_cols, 1)
    response = jnp.dot(
        schur_part,
        wanted.astype(jnp.float32),
        precision=lax.Precision.HIGHEST,
        preferred_element_type=jnp.float32,
    )
    partial_value = jnp.einsum(
        "rm,rc->mc",
        modes.astype(jnp.float32),
        response,
        precision=lax.Precision.HIGHEST,
        preferred_element_type=jnp.float32,
    )
    stiff_block = lax.psum_scatter(partial_value, "tile", scatter_dimension=0, tiled=True)
    picked = jnp.take(segment, gyro_rows, axis=0, mode="clip").astype(jnp.float32)
    gyro_block, spin_block = gyro_parts(
        picked,
        gyro_coupling,
        spin_softening,
        tile_pos * mode_rows_dev,
        mode_rows_dev,
        branch_pos * mode_cols,
        mode_cols,
    )
    return (schur_out, combine(stiff_block, gyro_block, spin_block, speed_index))


def gray(i):
    return i ^ (i >> 1)


def ring_z(place, k):
    return gray((gray(place[0] >> 1) + (4 - k)) & 3)


def block_at(place, j, k):
    return ring_z(place, k) * 2 + ((place[0] & 1) ^ j)


def keeps(place, k):
    return (ring_z(place, k) & 1) == (place[1] & 1)


def stays(place):
    return ((gray(place[0] >> 1) - gray(place[1])) & 1) == 0


IN_VMEM = pl.BlockSpec(memory_space=pltpu.VMEM)


def call(body, operands, outs, scratch=()):
    return pl.pallas_call(
        body,
        out_shape=[jax.ShapeDtypeStruct(shape, dtype) for shape, dtype in outs],
        in_specs=[pl.BlockSpec(memory_space=pltpu.SMEM)] + [IN_VMEM] * (len(operands) - 1),
        out_specs=[IN_VMEM] * len(outs),
        scratch_shapes=scratch,
        compiler_params=pltpu.CompilerParams(vmem_limit_bytes=GRANT),
        cost_estimate=pl.CostEstimate(flops=1 << 31, bytes_accessed=1 << 20, transcendentals=0),
    )(*operands)


def mul(left, right):
    return jnp.dot(left, right, preferred_element_type=jnp.float32)


def mul_wide(left, right):
    high = left.astype(jnp.bfloat16)
    low = (left - high.astype(jnp.float32)).astype(jnp.bfloat16)
    return mul(high, right) + mul(low, right)


ROW_STEPS = 2


def shares(place, stiffness, lower, blocks):
    rows = stiffness.shape[0]
    depth = lower.shape[1]
    cols = blocks[0][2][0].shape[1]
    step = rows // ROW_STEPS
    operands = [place, stiffness, lower]
    outs = []
    for _, _, pieces, old in blocks:
        operands += list(pieces) + ([] if old is None else [old])
        outs += [((rows, cols), jnp.float32)] * (1 if old is None else 2)

    def body(at, stiff, low, *refs):
        sources, targets = list(refs[: len(operands) - 3]), list(refs[len(operands) - 3 :])
        for j, k, pieces, old in blocks:
            uppers = [sources.pop(0) for _ in pieces]
            before = None if old is None else sources.pop(0)
            wanted = [targets.pop(0) for _ in range(1 if old is None else 2)]
            first_col = pl.multiple_of(block_at(at, j, k) * cols, cols)
            size = depth // len(pieces)

            @pl.loop(0, ROW_STEPS)
            def _(i):
                part = pl.ds(pl.multiple_of(i * step, step), step)
                value = stiff[part, pl.ds(first_col, cols)]
                for n, ref in enumerate(uppers):
                    value -= mul(low[part, n * size : (n + 1) * size], ref[:size, :])
                if before is None:
                    wanted[0][part, :] = value
                else:
                    sent, kept = wanted
                    keep_old = keeps(at, k - 2)
                    past = before[part, :]
                    sent[part, :] = jnp.where(keep_old, value, past)
                    kept[part, :] = jnp.where(keep_old, past, value)

    return call(body, operands, outs)


def fill_modes(at, target, near, beside, n):
    half, width = near.shape[1], target.shape[1]
    for other, source in enumerate((near, beside)):
        first = pl.multiple_of(((at[1] & 1) ^ other) * 2 * half, 2 * half)
        target[pl.ds(first, half), :] = source[n, :, :width]
        target[pl.ds(first + half, half), :] = source[n, :, width:]


def respond(place, groups, pairs, start, rows, mode_count):
    cols = pairs[0][3].shape[1]
    flat = [g for pair in groups for g in pair]
    shares_in = [s for p in pairs for s in p[3:]]
    plus = [] if start is None else [start]
    step = rows // ROW_STEPS

    def body(at, *refs):
        group_refs = refs[: len(flat)]
        share_refs = refs[len(flat) : len(flat) + len(shares_in)]
        out, scratch = refs[-2], refs[-1]
        for m, (older, newer, k, _, _) in enumerate(pairs):
            keep_old = keeps(at, k)

            def fill(slot, which):
                group, n = which
                fill_modes(at, scratch.at[slot], group_refs[2 * group], group_refs[2 * group + 1], n)

            @pl.when(keep_old)
            def _():
                fill(2 * m, newer)
                fill(2 * m + 1, older)

            @pl.when(jnp.logical_not(keep_old))
            def _():
                fill(2 * m, older)
                fill(2 * m + 1, newer)

        @pl.loop(0, ROW_STEPS)
        def _(i):
            part = pl.ds(pl.multiple_of(i * step, step), step)
            if plus:
                total = refs[len(flat) + len(shares_in)][part, :]
            else:
                total = jnp.zeros((step, mode_count), jnp.float32)
            for n in range(len(shares_in)):
                total += mul_wide(share_refs[n][part, :], scratch[n])
            out[part, :] = total

    return call(
        body,
        [place] + flat + shares_in + plus,
        [((rows, mode_count), jnp.float32)],
        [pltpu.VMEM((len(shares_in), cols, mode_count), jnp.bfloat16)],
    )[0]


def reduce_modes(place, groups, pair, response, modes, branches, tiles):
    mode_count = modes.shape[1]
    group = mode_count // tiles // 2
    older, newer, k, sent, kept = pair
    rows, cols = sent.shape
    flat = [g for both in groups for g in both]

    def body(at, *refs):
        group_refs = refs[: len(flat)]
        sent_ref, kept_ref, resp, mode, pieces, scratch = refs[len(flat) :]
        keep_old = keeps(at, k)

        def fill(slot, which):
            fill_modes(
                at, scratch.at[slot], group_refs[2 * which[0]], group_refs[2 * which[0] + 1], which[1]
            )

        @pl.when(keep_old)
        def _():
            fill(0, newer)
            fill(1, older)

        @pl.when(jnp.logical_not(keep_old))
        def _():
            fill(0, older)
            fill(1, newer)

        total = resp[...] + mul_wide(sent_ref[...], scratch[0]) + mul_wide(kept_ref[...], scratch[1])
        high = total.astype(jnp.bfloat16)
        rest = (total - high.astype(jnp.float32)).astype(jnp.bfloat16)
        across = (((0,), (0,)), ((), ()))
        reduced = lax.dot_general(
            mode[...], high, across, preferred_element_type=jnp.float32
        ) + lax.dot_general(mode[...], rest, across, preferred_element_type=jnp.float32)
        split = reduced.reshape(tiles, 2, group, mode_count)
        upper = split[:, 0].reshape(tiles * group, mode_count)
        under = split[:, 1].reshape(tiles * group, mode_count)
        left = lax.broadcasted_iota(jnp.int32, (tiles * group, 128), 1) < 64
        for half in range(branches // 2):
            u = upper[:, 128 * half : 128 * half + 128]
            v = under[:, 128 * half : 128 * half + 128]
            pieces[2 * half] = jnp.where(left, u, pltpu.roll(v, 64, 1))
            pieces[2 * half + 1] = jnp.where(left, pltpu.roll(u, 64, 1), v)

    return call(
        body,
        [place] + flat + [sent, kept, response, modes],
        [((branches, tiles * group, 128), jnp.float32)],
        [pltpu.VMEM((2, cols, mode_count), jnp.bfloat16)],
    )[0]


def pick(which, arrays):
    value = arrays[-1]
    for n in range(len(arrays) - 2, -1, -1):
        value = jnp.where(which == n, arrays[n], value)
    return value


def to_wire(value):
    return (value * SHARE_SCALE).astype(jnp.float16)


def from_wire(value):
    return value.astype(jnp.float32) * (1.0 / SHARE_SCALE)


def shards_ring(
    interface_stiffness,
    lower_factor,
    upper_factor,
    modes,
    gyro_rows,
    gyro_coupling,
    spin_softening,
    speed_index,
):
    f32 = jnp.float32
    tiles = lax.axis_size("tile")
    branches = lax.axis_size("subtree")
    tile = lax.axis_index("tile")
    branch = lax.axis_index("subtree")
    place = jnp.stack([tile, branch]).astype(jnp.int32)
    stiffness = interface_stiffness[0]
    lower = lower_factor[0]
    upper = upper_factor[0]
    rows = stiffness.shape[0]
    depth, cols = upper.shape
    mode_count = modes.shape[1]

    def ring_pairs(turn):
        return [
            (gray(p) * 2 + a, gray((p + 1) % 4) * 2 + a)
            if turn
            else (gray((p + 1) % 4) * 2 + 1 - a, gray(p) * 2 + a)
            for p in range(4)
            for a in range(2)
        ]

    def over_z(block):
        return lax.ppermute(block, "tile", ring_pairs(True))

    def over_x(block):
        return lax.ppermute(block, "tile", [(i, i ^ 1) for i in range(tiles)])

    def over_y(block):
        return lax.ppermute(block, "subtree", [(i, i ^ 2) for i in range(branches)])

    def over_core(block):
        return lax.ppermute(block, "subtree", [(i, i ^ 1) for i in range(branches)])

    def over_y_of(block, first):
        route = [
            (b * tiles + t, (b ^ 2) * tiles + t)
            for b in range(branches)
            for t in range(tiles)
            if stays((t, b)) != first
        ]
        return lax.ppermute(block, ("subtree", "tile"), route)

    chunk = modes.shape[0] // 2
    mine = lax.dynamic_slice_in_dim(modes, (branch & 1) * chunk, chunk, 0)
    mine = jnp.concatenate([mine[: chunk // 2], mine[chunk // 2 :]], axis=1)
    load = jnp.concatenate([upper, mine], axis=0)
    mode_far = lax.ppermute(mine, "tile", ring_pairs(False))
    z1, x0 = lax.optimization_barrier((over_z(load), over_x(load)))
    z2, x1 = lax.optimization_barrier((over_z(z1), over_x(z1)))
    z3, x2 = lax.optimization_barrier((over_z(z2), over_x(z2)))
    cut = depth // 2
    x3_low, x3_high = over_x(z3[:cut]), over_z(x2[cut:depth])

    def spread(pieces):
        near = jnp.stack(pieces)
        return near, over_core(near)

    early = spread([mine, z1[depth:], x0[depth:], mode_far])
    middle = spread([z2[depth:], x1[depth:]])
    late = spread([z3[depth:], x2[depth:]])
    early_n, middle_n, late_n = 0, 1, 2
    groups = [early, middle, late]

    (p00,) = shares(place, stiffness, lower, [(0, 0, [load], None)])
    p01, p10 = shares(place, stiffness, lower, [(0, 1, [z1], None), (1, 0, [x0], None)])
    sent_a0, kept_a0, p11 = shares(
        place, stiffness, lower, [(0, 2, [z2], p00), (1, 1, [x1], None)]
    )
    sent_b0, kept_b0, sent_a1, kept_a1 = shares(
        place, stiffness, lower, [(0, 3, [z3], p01), (1, 2, [x2], p10)]
    )
    chip_a0 = kept_a0 + over_core(sent_a0)
    came_a0 = over_y_of(to_wire(chip_a0), True)
    chip_b0 = kept_b0 + over_core(sent_b0)
    wire_b0 = to_wire(chip_b0)
    came_b0 = over_y_of(wire_b0, False)
    chip_a1 = kept_a1 + over_core(sent_a1)
    wire_a1 = to_wire(chip_a1)
    came_a1 = over_y_of(wire_a1, True)

    pair_a0 = ((early_n, 0), (middle_n, 0), 0, sent_a0, kept_a0)
    pair_b0 = ((early_n, 1), (late_n, 0), 1, sent_b0, kept_b0)
    pair_a1 = ((early_n, 2), (late_n, 1), 0, sent_a1, kept_a1)
    response = respond(place, [early, middle], [pair_a0], None, rows, mode_count)
    response = respond(place, groups, [pair_b0, pair_a1], response, rows, mode_count)
    x3_low, x3_high, came_a0, _, _ = lax.optimization_barrier(
        (x3_low, x3_high, came_a0, wire_b0, wire_a1)
    )
    sent_b1, kept_b1 = shares(place, stiffness, lower, [(1, 3, [x3_low, x3_high], p11)])

    mode_rows = mode_count // tiles
    mode_cols = mode_count // branches
    pair_b1 = ((0, 0), (0, 1), 1, sent_b1, kept_b1)
    last_two = (
        jnp.stack([middle[0][1], early[0][3]]),
        jnp.stack([middle[1][1], early[1][3]]),
    )
    pieces = reduce_modes(place, [last_two], pair_b1, response, modes, branches, tiles)
    pieces = pieces.reshape(branches * tiles, mode_rows // 2, 2 * mode_cols)
    pieces, gyro_rows = lax.optimization_barrier((pieces, gyro_rows))
    summed = jnp.sum(lax.all_to_all(pieces, ("subtree", "tile"), 0, 0), axis=0)
    stiff_block = jnp.concatenate([summed[:, :mode_cols], summed[:, mode_cols:]], axis=0)

    chip_b1 = kept_b1 + over_core(sent_b1)
    wire_b1, came_a1, came_b0 = lax.optimization_barrier((to_wire(chip_b1), came_a1, came_b0))
    came_b1 = over_y_of(wire_b1, False)
    here = stays((tile, branch))
    left = tile & 1
    first = jnp.where(here, chip_a0 + from_wire(came_a0), chip_b0 + from_wire(came_b0))
    ready = jnp.concatenate([first, first], axis=1)
    second = jnp.where(here, chip_a1 + from_wire(came_a1), chip_b1 + from_wire(came_b1))
    schur_out = lax.dynamic_update_slice_in_dim(ready, second, (1 - left) * cols, 1)

    row_tile, row_in = gyro_rows // modes.shape[0], gyro_rows % modes.shape[0]
    turn = (gray(tile // 2) - gray(row_tile // 2)) & 3
    index = ((row_tile ^ tile) & 1) * 4 + turn
    block = pick(index, [0, 1, 4, 6, 2, 5, 7, 3])
    half_row = row_in % chunk
    table = jnp.concatenate([g[side] for side in range(2) for g in groups]).reshape(
        -1, 2 * mode_count
    )
    line = (((row_in // chunk) ^ branch) & 1) * 8 + block
    wide = jnp.take(
        table, line * (chunk // 2) + half_row % (chunk // 2), axis=0, mode="clip"
    )
    picked = jnp.where(
        (half_row < chunk // 2)[:, None], wide[:, :mode_count], wide[:, mode_count:]
    ).astype(f32)
    gyro_block, spin_block = gyro_parts(
        picked,
        gyro_coupling,
        spin_softening,
        tile * mode_rows,
        mode_rows,
        branch * mode_cols,
        mode_cols,
    )
    return (schur_out, combine(stiff_block, gyro_block, spin_block, speed_index))


def solution(mesh):
    placed = (
        P("subtree", "tile", None),
        P("subtree", "tile", None),
        P("subtree", None, "tile"),
        P("tile", None),
        P(),
        P(),
        P(),
        P(),
    )
    ring = (mesh.shape["subtree"], mesh.shape["tile"]) == (4, 8)
    return jax.shard_map(
        shards_ring if ring else shards_any,
        mesh=mesh,
        in_specs=placed,
        out_specs=(P("tile", "subtree"), P(None, "tile", "subtree")),
        check_vma=False,
    )
```
